32 devices in a mesh: gx: 4 (over z), gy: 4 (over x, core), gz: 2 (over y).
Axes of the slice: x: 2, y: 2, z: 4, core: 2. Of those that a mesh axis runs over, the one named last changes fastest.
Arguments:
- phase: int32 [4, 8, 64], P('gx', 'gy', 'gz'), may hold values from 0 to 1
- lame: float32 [2, 2], replicated, may hold values from 0.3 to 10
- start: float32 [3, 32, 16, 32, 256], P(None, None, 'gx', 'gy', 'gz'), may hold values from -6 to 6
Outputs:
- basis: float32 [3, 32, 16, 32, 256], P(None, None, 'gx', 'gy', 'gz')
- coarse: float32 [32, 32], replicated
The draws below stay inside these ranges and needn't reach their ends.
All inputs are finite; a program needn't handle non-finite values.
Results may differ from the reference program's by a relative error of at most 0.0001.
Values sent between devices are 32-bit elements; how exact they have to be, the bound alone decides.
A program may use at most 64 MiB of HBM per device.

```python
import math
import jax
import jax.numpy as jnp
from jax import lax

VECS = 32
ITERS = 3
PHASES = 2
BRICK = 4
NX = 16
NY = 32
NZ = 256


def touch_ends(array, rng, low, high):
    place = [jax.random.randint(jax.random.fold_in(rng, axis), (), 0, length) for axis, length in enumerate(array.shape)]
    widest = array.shape.index(max(array.shape))
    next_to = place[:widest] + [(place[widest] + 1) % array.shape[widest]] + place[widest + 1:]
    return array.at[tuple(place)].set(low).at[tuple(next_to)].set(high)


def steps_of(own_key, dims, pieces, low, top_value):
    def one(axis_at, blocks):
        draws = jax.random.uniform(jax.random.fold_in(jax.random.fold_in(own_key, 6), axis_at), (blocks,), jnp.float32, low / len(pieces), top_value / len(pieces))
        return jnp.repeat(jnp.exp(draws), dims[axis_at] // blocks).reshape((-1,) + (1,) * (len(dims) - axis_at - 1))

    gain = one(*pieces[0])
    for cut in pieces[1:]:
        gain = gain * one(*cut)
    return gain


def normal_values(key, shape, spread, reach, split=(), kind=jnp.bfloat16):
    values = jax.random.normal(key, shape, jnp.float32) * spread
    if len(split) > 0:
        values = steps_of(key, shape, split, -0.22, 0.18) * values
    return jnp.clip(values, min=-reach, max=reach).astype(kind)


def setup_inputs(seed: int = 0) -> dict:
    key_list = jax.random.split(jax.random.key(seed), 4)
    phase = touch_ends(jax.random.randint(key_list[0], (NX // BRICK, NY // BRICK, NZ // BRICK), 0, PHASES), jax.random.fold_in(key_list[0], 1), 0, PHASES - 1).astype(jnp.int32)
    lame = jnp.clip(jnp.exp(jax.random.uniform(key_list[1], (PHASES, 2), jnp.float32, math.log(0.3), math.log(10.0))), 0.3, 10.0)
    start = normal_values(key_list[2], (3, VECS, NX, NY, NZ), 1.0, 6.0, ((2, 4), (3, 4), (4, 2)), jnp.float32)
    return dict(phase=phase, lame=lame, start=start)


def node_fields(padded_bricks, lame):
    nodes = jnp.repeat(jnp.repeat(jnp.repeat(padded_bricks, BRICK, 0), BRICK, 1), BRICK, 2)
    cut = BRICK - 1
    nodes = nodes[cut:-cut, cut:-cut, cut:-cut]
    shear = jnp.zeros(nodes.shape, jnp.float32)
    first = jnp.zeros(nodes.shape, jnp.float32)
    for index in range(PHASES):
        hit = nodes == index
        shear = shear + jnp.where(hit, lame[index, 0], 0.0)
        first = first + jnp.where(hit, lame[index, 1], 0.0)
    return (shear, first + shear)

def stencil(padded, shear, grow):
    centre = padded[:, :, 1:-1, 1:-1, 1:-1]
    shear_c = shear[1:-1, 1:-1, 1:-1]
    grow_c = grow[1:-1, 1:-1, 1:-1]
    total = jnp.zeros(centre.shape, centre.dtype)
    for axis_d in range(3):
        length = centre.shape[2 + axis_d]
        for offset in (0, 2):
            cuts = [slice(1, -1), slice(1, -1), slice(1, -1)]
            cuts[axis_d] = slice(offset, offset + length)
            cuts = tuple(cuts)
            beside = padded[(slice(None), slice(None)) + cuts]
            w_shear = 0.5 * (shear_c + shear[cuts])
            w_grow = 0.5 * (grow_c + grow[cuts])
            weight = jnp.stack([w_shear + w_grow if comp == axis_d else w_shear for comp in range(3)])
            total = total + weight[:, None] * (centre - beside)
    return total

def inner(left, right):
    return jnp.einsum('ckxyz,clxyz->kl', left, right, precision=lax.Precision.HIGHEST)

def inverse_factor(gram):
    lower_f = jnp.linalg.cholesky(gram)
    return lax.linalg.triangular_solve(lower_f, jnp.eye(gram.shape[0], dtype=jnp.float32), left_side=True, lower=True)

def reference(phase, lame, start):
    total_rows = 3.0 * start.shape[2] * start.shape[3] * start.shape[4]
    shear, grow = node_fields(jnp.pad(phase, 1), lame)
    widths = ((0, 0), (0, 0), (1, 1), (1, 1), (1, 1))
    block = start
    for step in range(ITERS):
        image = stencil(jnp.pad(block, widths), shear, grow)
        factor = inverse_factor(inner(image, image) / total_rows)
        block = jnp.einsum('kl,clxyz->ckxyz', factor, image, precision=lax.Precision.HIGHEST)
    applied = stencil(jnp.pad(block, widths), shear, grow)
    return (block, inner(block, applied) / total_rows)
```

```python
import functools

import jax
import jax.numpy as jnp
from jax import lax
from jax.experimental import pallas as pl
from jax.experimental.pallas import tpu as pltpu
from jax.sharding import PartitionSpec as P

ITERS = 3
PHASES = 2
BRICK = 4
LAG = 1
GROUP = 8
PANEL = 8
AXES = ("gx", "gy", "gz")
MESH = pl.DeviceIdType.MESH
F32 = jnp.float32
BF16 = jnp.bfloat16


def split(value, count):
    pieces = []
    for _ in range(count):
        piece = value.astype(BF16)
        pieces.append(piece)
        value = value - piece.astype(F32)
    return pieces


def contract_last(left, right):
    return lax.dot_general(
        left, right, (((1,), (1,)), ((), ())), preferred_element_type=F32
    )


def matmul(left, right):
    return jnp.dot(left, right, preferred_element_type=F32)


def inverse_factor(gram, size):
    row = lax.broadcasted_iota(jnp.int32, (size, size), 0)
    col = lax.broadcasted_iota(jnp.int32, (size, size), 1)
    both = jnp.concatenate([gram, jnp.where(row == col, 1.0, 0.0).astype(F32)], axis=1)
    rows = lax.broadcasted_iota(jnp.int32, both.shape, 0)
    for first in range(0, size, PANEL):
        columns = [
            jnp.broadcast_to(both[:, j : j + 1], both.shape)
            for j in range(first, first + PANEL)
        ]
        for t in range(PANEL):
            j = first + t
            scale = lax.rsqrt(columns[t][j : j + 1])
            column = columns[t] * scale
            pivot = both[j : j + 1] * scale
            below = jnp.where(rows > j, column, 0.0)
            both = jnp.where(rows == j, pivot, both - below * pivot)
            for u in range(t + 1, PANEL):
                columns[u] = columns[u] - column * column[first + u : first + u + 1]
    return both[:, size:]


def kernel(
    counts,
    dims,
    lame_in,
    phase_hbm,
    start,
    stage,
    mixing_out,
    form_out,
    lame,
    phase,
    field,
    plane_in,
    row_in,
    edge_out,
    edge_in,
    phase_own,
    phase_in,
    weights,
    parts,
    image_parts,
    total_sum,
    sums,
    local_sem,
    phase_send,
    phase_recv,
    send_sem,
    recv_sem,
    sum_send,
    sum_recv,
):
    comps, vecs, nx, ny, nz = dims
    total_rows = 1.0 * comps * nx * ny * nz * counts[0] * counts[1] * counts[2]
    me = [lax.axis_index(axis) for axis in AXES]
    tall, wide = vecs * ny, nx * nz
    pairs = nz // 2
    packs = vecs * nx // pairs
    per = vecs // packs

    sizes = (counts[1] * counts[2], counts[0])
    places = (me[1] * counts[2] + me[2], me[0])
    offsets = (0, sizes[0])

    def member(stage_at, k):
        if stage_at == 1:
            return {"gx": k}
        return {"gy": lax.div(k, counts[2]), "gz": lax.rem(k, counts[2])}

    def each_other(stage_at, action):
        def one(step, _):
            action(lax.rem(places[stage_at] + step, sizes[stage_at]))
            return 0

        lax.fori_loop(1, sizes[stage_at], one, 0)

    barrier = pltpu.get_barrier_semaphore()
    for stage_at in (1, 0):
        each_other(
            stage_at,
            lambda k: pl.semaphore_signal(
                barrier, inc=1, device_id=member(stage_at, k), device_id_type=MESH
            ),
        )

    small = [
        pltpu.make_async_copy(phase_hbm, phase, local_sem.at[comps * nx]),
        pltpu.make_async_copy(lame_in, lame, local_sem.at[comps * nx + 1]),
    ]
    for copy in small:
        copy.start()

    def load_copy(c, x):
        return pltpu.make_async_copy(
            start.at[c, :, x], field.at[0, c, x], local_sem.at[c * nx + x]
        )

    def load(k, _):
        load_copy(lax.div(k, nx), lax.rem(k, nx)).start()
        return 0

    lax.fori_loop(0, comps * nx, load, 0)

    def has(side):
        axis = side // 2
        return me[axis] > 0 if side % 2 == 0 else me[axis] < counts[axis] - 1

    def lacks(side):
        axis = side // 2
        return me[axis] == 0 if side % 2 == 0 else me[axis] == counts[axis] - 1

    def beside(side):
        axis = side // 2
        return {AXES[axis]: me[axis] - 1 if side % 2 == 0 else me[axis] + 1}

    plane = jnp.zeros((ny, nz), F32)
    for side in range(2):

        def leave_out(v, _, side=side):
            for c in range(comps):
                plane_in[ITERS, c, side, v] = plane
            return 0

        lax.fori_loop(0, vecs, leave_out, 0)

        @pl.when(lacks(side))
        def _(side=side):
            def clear(v, _):
                for s in range(ITERS):
                    for c in range(comps):
                        plane_in[s, c, side, v] = plane
                return 0

            lax.fori_loop(0, vecs, clear, 0)

        @pl.when(lacks(2 + side))
        def _(side=side):
            def clear(k, _):
                s, c = lax.div(k, comps), lax.rem(k, comps)
                row_in[s, c, side] = jnp.zeros((nx, vecs, nz), F32)
                return 0

            lax.fori_loop(0, (ITERS + 1) * comps, clear, 0)

        @pl.when(lacks(4 + side))
        def _(side=side):
            def clear(k, _):
                s, c = lax.div(k, comps), lax.rem(k, comps)
                edge_in[s, c, side] = jnp.zeros((packs, ny, nz), F32)
                return 0

            lax.fori_loop(0, (ITERS + 1) * comps, clear, 0)

    for side in range(6):

        @pl.when(lacks(side))
        def _(side=side):
            phase_in[side] = jnp.zeros(phase_in.shape[1:], F32)

    for copy in small:
        copy.wait()
    bricks_x, bricks_y, bricks_z = phase.shape
    spread = jnp.where(
        lax.broadcasted_iota(jnp.int32, (bricks_z, nz), 1) // BRICK
        == lax.broadcasted_iota(jnp.int32, (bricks_z, nz), 0),
        1.0,
        0.0,
    ).astype(F32)
    row_brick = lax.broadcasted_iota(jnp.int32, (ny, bricks_z), 0) // BRICK
    for bx in range(bricks_x):
        own = phase[bx].astype(F32)
        rows = jnp.zeros((ny, bricks_z), F32)
        for by in range(bricks_y):
            rows = jnp.where(
                row_brick == by,
                jnp.broadcast_to(own[by : by + 1], (ny, bricks_z)),
                rows,
            )
        phase_own[bx] = jnp.dot(rows, spread, preferred_element_type=F32)

    def upward(c):
        return lax.rem(me[1] + c, 2) == 0

    def face(s, c, side, first=False):
        if side < 2:
            x = 0 if side == 0 else nx - 1
            src = start.at[c, :, x] if first else field.at[s, c, x]
            level = 0 if first else jnp.where(s == ITERS, ITERS + 1, s)
            dst = plane_in.at[level, c, 1 - side]
        elif side < 4:
            src = field.at[s, c, :, :, 0 if side == 2 else ny - 1]
            dst = row_in.at[s, c, 3 - side]
        else:
            src, dst = edge_out.at[s, c], edge_in.at[s, c, 5 - side]
        return src, dst

    def send_copy(s, c, side, first=False):
        src, dst = face(s, c, side, first)
        return pltpu.make_async_remote_copy(
            src_ref=src,
            dst_ref=dst,
            send_sem=send_sem.at[s, c, side],
            recv_sem=recv_sem.at[s, c, side ^ 1],
            device_id=beside(side),
            device_id_type=MESH,
        )

    def recv_copy(s, c, side):
        src, dst = face(s, c, side ^ 1)
        return pltpu.make_async_remote_copy(
            src_ref=src,
            dst_ref=dst,
            send_sem=send_sem.at[s, c, side],
            recv_sem=recv_sem.at[s, c, side],
            device_id=beside(side),
            device_id_type=MESH,
        )

    def sends(s, c, side):
        if side >= 2:
            return has(side)
        way = upward(c) if side == 1 else jnp.logical_not(upward(c))
        return has(side) & ((s < ITERS) | way)

    def send(s, c, sides, first=False):
        for side in sides:

            @pl.when(has(side) if first else sends(s, c, side))
            def _(side=side):
                send_copy(s, c, side, first).start()

    def receive(s, c, sides):
        for side in sides:

            @pl.when(has(side))
            def _(side=side):
                recv_copy(s, c, side).wait_recv()

    def phase_copy(side, signal):
        return pltpu.make_async_remote_copy(
            src_ref=phase_own,
            dst_ref=phase_in.at[signal],
            send_sem=phase_send.at[side],
            recv_sem=phase_recv.at[signal],
            device_id=beside(side),
            device_id_type=MESH,
        )

    lane = lax.broadcasted_iota(jnp.int32, (ny, nz), 1)
    line = lax.broadcasted_iota(jnp.int32, (ny, nz), 0)
    pair = lax.rem(lax.div(lane + 1, 2), pairs)

    turned = lax.rem(lane + 1, nz)

    def side_by_side(values, width):
        total = None
        for k, value in enumerate(values):
            if total is None:
                total = value
            else:
                moved = pltpu.roll(value, k * width, 1)
                total = jnp.where(turned < k * width, total, moved)
        return total

    def edges_of(s, c):
        for e in range(packs):
            blocks = []
            for first in range(0, pairs, GROUP):
                values = []
                for m in range(first, first + GROUP):
                    values.append(field[s, c, m % nx, e * per + m // nx])
                blocks.append(side_by_side(values, 2))
            edge_out[s, c, e] = side_by_side(blocks, 2 * GROUP)

    pl.semaphore_wait(barrier, sizes[0] + sizes[1] - 2)

    def first_planes(c, _):
        send(0, c, range(2), True)
        return 0

    lax.fori_loop(0, comps, first_planes, 0)
    for side in range(6):

        @pl.when(has(side))
        def _(side=side):
            phase_copy(side, side ^ 1).start()

    def first_edges(c, _):
        for x in range(nx):
            load_copy(c, x).wait()
        send(0, c, range(2, 4))

        edges_of(0, c)
        send(0, c, range(4, 6))
        return 0

    lax.fori_loop(0, comps, first_edges, 0)

    for side in range(6):

        @pl.when(has(side))
        def _(side=side):
            phase_copy(side, side).wait_recv()

    def material(kinds):
        shear = jnp.zeros(kinds.shape, F32)
        first = jnp.zeros(kinds.shape, F32)
        for index in range(PHASES):
            hit = kinds == float(index)
            shear = shear + jnp.where(hit, lame[index, 0], 0.0)
            first = first + jnp.where(hit, lame[index, 1], 0.0)
        return shear, first + shear

    for x in range(nx):
        bx = x // BRICK
        own = phase_own[bx]
        others = [
            phase_own[(x - 1) // BRICK] if x > 0 else phase_in[0, bricks_x - 1],
            phase_own[(x + 1) // BRICK] if x < nx - 1 else phase_in[1, 0],
            pltpu.roll(jnp.where(line == ny - 1, phase_in[2, bx], own), 1, 0),
            pltpu.roll(jnp.where(line == 0, phase_in[3, bx], own), ny - 1, 0),
            pltpu.roll(jnp.where(lane == nz - 1, phase_in[4, bx], own), 1, 1),
            pltpu.roll(jnp.where(lane == 0, phase_in[5, bx], own), nz - 1, 1),
        ]
        shear_c, grow_c = material(own)
        total = [None] * comps
        for side in range(6):
            shear_n, grow_n = material(others[side])
            w_shear = 0.5 * (shear_c + shear_n)
            w_grow = 0.5 * (grow_c + grow_n)
            for c in range(comps):
                w = w_shear + w_grow if side // 2 == c else w_shear
                weights[c, x, side] = w
                total[c] = w if total[c] is None else total[c] + w
        for c in range(comps):
            weights[c, x, 6] = total[c]

    def image(s, c, v, edges, at):
        value = [plane_in[s, c, 0, v]]
        value += [field[s, c, x, v] for x in range(nx)]
        value += [plane_in[s, c, 1, v]]
        totals = []
        for x in range(nx):
            centre = value[x + 1]
            shift = 2 * (at * nx + x)
            border = pltpu.roll(edges, nz - shift, 1) if shift else edges
            low = jnp.broadcast_to(row_in[s, c, 0, x, pl.ds(v, 1), :], (ny, nz))
            high = jnp.broadcast_to(row_in[s, c, 1, x, pl.ds(v, 1), :], (ny, nz))
            others = [
                value[x],
                value[x + 2],
                jnp.where(line == 0, low, pltpu.roll(centre, 1, 0)),
                jnp.where(line == ny - 1, high, pltpu.roll(centre, ny - 1, 0)),
                jnp.where(lane == 0, border, pltpu.roll(centre, 1, 1)),
                jnp.where(lane == nz - 1, border, pltpu.roll(centre, nz - 1, 1)),
            ]
            total = weights[c, x, 6] * centre
            for side in range(6):
                total = total - weights[c, x, side] * others[side]
            totals.append(total)
        return totals

    def apply(s, c):
        def step(e, _):
            edges = jnp.where(
                lax.rem(lane, 2) == 0,
                pltpu.roll(edge_in[s, c, 0, e], 1, 1),
                pltpu.roll(edge_in[s, c, 1, e], nz - 1, 1),
            )
            for at in range(per):
                v = e * per + at
                out = image(s, c, v, edges, at)
                for x in range(nx):
                    field[s + 1, c, x, v] = out[x]
            return 0

        lax.fori_loop(0, packs, step, 0)

    def put_parts(s, c, ref):
        for x in range(nx):
            high, low = split(field[s, c, x].reshape(tall, nz), 2)
            ref[0, :, x * nz : (x + 1) * nz] = high
            ref[1, :, x * nz : (x + 1) * nz] = low

    def sum_copy(which, stage_at, slot, other):
        at = offsets[stage_at] + slot
        return pltpu.make_async_remote_copy(
            src_ref=sums.at[which, at],
            dst_ref=sums.at[which, at],
            send_sem=sum_send.at[which, offsets[stage_at] + other],
            recv_sem=sum_recv.at[which, at],
            device_id=member(stage_at, other),
            device_id_type=MESH,
        )

    def sum_start(which, stage_at, value):
        mine = places[stage_at]
        sums[which, offsets[stage_at] + mine] = value
        each_other(stage_at, lambda k: sum_copy(which, stage_at, mine, k).start())

    def sum_end(which, stage_at):
        each_other(stage_at, lambda k: sum_copy(which, stage_at, k, k).wait_recv())
        total = sums[which, offsets[stage_at]]
        for k in range(1, sizes[stage_at]):
            total = total + sums[which, offsets[stage_at] + k]
        return total

    down_n = sums.shape[2]
    across_n = vecs // down_n

    def fold(acc):
        keep = (
            lax.broadcasted_iota(jnp.int32, (vecs, ny, tall), 1)
            == lax.broadcasted_iota(jnp.int32, (vecs, ny, tall), 2) % ny
        )
        rows = jnp.sum(jnp.where(keep, acc.reshape(vecs, ny, tall), 0.0), axis=1)
        flat = jnp.concatenate(
            [rows[k * down_n : (k + 1) * down_n] for k in range(across_n)], axis=1
        )
        pieces = jnp.concatenate([p.astype(F32) for p in split(flat, 3)], axis=0)
        source = lax.broadcasted_iota(jnp.int32, (across_n * tall, across_n * vecs), 0)
        target = lax.broadcasted_iota(jnp.int32, (across_n * tall, across_n * vecs), 1)
        to = jnp.where(source // ny == target, 1.0, 0.0).astype(BF16)
        out = matmul(pieces.astype(BF16), to)
        return out[:down_n] + out[down_n : 2 * down_n] + out[2 * down_n :]

    def unpacked(value):
        pieces = [value[:, k * vecs : (k + 1) * vecs] for k in range(across_n)]
        square = jnp.concatenate(pieces, axis=0)
        return 0.5 * (square + square.T)

    def advance(s, c):
        receive(s, c, range(6))
        apply(s, c)
        send(s + 1, c, range(4))
        edges_of(s + 1, c)
        send(s + 1, c, range(4, 6))

    def early(k, _):
        advance(lax.div(k, comps), lax.rem(k, comps))
        return 0

    def gram_of(c):
        put_parts(ITERS, c, parts.at[c])
        side = contract_last(parts[c, 0], parts[c, 1])
        total_sum[0] += contract_last(parts[c, 0], parts[c, 0]) + (side + side)

    def form_of(c):
        receive(ITERS, c, range(2, 6))
        apply(ITERS, c)
        put_parts(ITERS + 1, c, image_parts)
        more = contract_last(parts[c, 0], image_parts[0])
        more = more + contract_last(parts[c, 1], image_parts[0])
        total_sum[1] += more + contract_last(parts[c, 0], image_parts[1])

    lax.fori_loop(0, (ITERS - 1) * comps, early, 0)
    total_sum[...] = jnp.zeros(total_sum.shape, F32)

    def last(k, _):
        @pl.when(k < comps)
        def _():
            advance(ITERS - 1, k)
            gram_of(k)

        @pl.when(k == comps - 1)
        def _():
            sum_start(0, 0, fold(total_sum[0]))

        @pl.when(k >= LAG)
        def _():
            form_of(k - LAG)

        return 0

    lax.fori_loop(0, comps + LAG, last, 0)
    sum_start(0, 1, sum_end(0, 0))

    def cut(c, _):
        way = upward(c)
        side = jnp.where(way, 0, 1)
        x = jnp.where(way, 0, nx - 1)

        @pl.when(jnp.where(way, me[0], counts[0] - 1 - me[0]) > 0)
        def _():
            pltpu.make_async_remote_copy(
                src_ref=field.at[ITERS, c, 0],
                dst_ref=plane_in.at[ITERS + 1, c, side],
                send_sem=send_sem.at[ITERS, c, side],
                recv_sem=recv_sem.at[ITERS, c, side],
                device_id={"gx": me[0] + 1 - 2 * jnp.where(way, 1, 0)},
                device_id_type=MESH,
            ).wait_recv()
            there = plane_in[ITERS + 1, c, side] * (-2.0 * weights[c, x, side])
            high, low = split(there.reshape(tall, nz), 2)
            here = pl.ds(pl.multiple_of(x * nz, nz), nz)
            own = [parts[c, p, :, here] for p in range(2)]
            more = contract_last(own[0], high) + contract_last(own[1], high)
            total_sum[1] += more + contract_last(own[0], low)

        return 0

    lax.fori_loop(0, comps, cut, 0)
    sum_start(1, 0, fold(total_sum[1]))
    gram = sum_end(0, 1)
    sum_start(1, 1, sum_end(1, 0))
    mixing = inverse_factor(unpacked(gram) / total_rows, vecs)
    mixing_out[...] = mixing

    widen = jnp.where(
        lax.broadcasted_iota(jnp.int32, (vecs, tall), 0)
        == lax.broadcasted_iota(jnp.int32, (vecs, tall), 1) // ny,
        1.0,
        0.0,
    ).astype(BF16)
    same = (
        lax.broadcasted_iota(jnp.int32, (tall, tall), 0) % ny
        == lax.broadcasted_iota(jnp.int32, (tall, tall), 1) % ny
    )
    mixers = []
    for piece in split(mixing, 2):
        tallest = jnp.broadcast_to(piece.astype(F32)[:, None, :], (vecs, ny, vecs))
        big = matmul(tallest.reshape(tall, vecs).astype(BF16), widen)
        mixers.append(jnp.where(same, big, 0.0).astype(BF16))
    for p in range(2):
        image_parts[p, :, :tall] = mixers[p]

    def mix(c, _):
        for x in range(0, nx, 2):
            high, low = (parts[c, p, :, x * nz : (x + 2) * nz] for p in range(2))
            left = [image_parts[p, :, :tall] for p in range(2)]
            out = matmul(left[0], high) + matmul(left[1], high)
            out = out + matmul(left[0], low)
            for t in range(2):
                stage[c, :, x + t] = out[:, t * nz : (t + 1) * nz].reshape(vecs, ny, nz)
        return 0

    lax.fori_loop(0, comps, mix, 0)
    form_out[...] = unpacked(sum_end(1, 1))

    def sent(k, _):
        s, c = lax.div(k, comps), lax.rem(k, comps)
        for side in range(6):

            @pl.when(sends(s, c, side))
            def _(side=side):
                send_copy(s, c, side).wait_send()

        return 0

    lax.fori_loop(0, (ITERS + 1) * comps, sent, 0)
    for side in range(6):

        @pl.when(has(side))
        def _(side=side):
            phase_copy(side, side ^ 1).wait_send()

    for which in range(2):
        for stage_at in range(2):
            each_other(
                stage_at,
                lambda k: sum_copy(which, stage_at, places[stage_at], k).wait_send(),
            )


def finish(total_rows, stage, mixing, form, basis, coarse, sem):
    copy = pltpu.make_async_copy(stage, basis, sem)
    copy.start()
    exact = lax.Precision.HIGHEST
    left = mixing[...]
    first = jnp.dot(left, form[...], precision=exact, preferred_element_type=F32)
    coarse[...] = (
        lax.dot_general(
            first,
            left,
            (((1,), (1,)), ((), ())),
            precision=exact,
            preferred_element_type=F32,
        )
        / total_rows
    )
    copy.wait()


def on_device(counts, phase, lame, start):
    comps, vecs, nx, ny, nz = dims = start.shape
    packs = 2 * vecs * nx // nz
    tall, wide = vecs * ny, nx * nz
    assert comps == 3 and nx % 2 == 0 and ny == 8 and nz % 128 == 0
    assert (nz // 2) % GROUP == 0 and vecs % PANEL == 0
    assert packs * nz == 2 * vecs * nx and vecs % (2 * packs) == 0
    slots = counts[0] + counts[1] * counts[2]
    steps = ITERS + 1
    total_rows = 1.0 * comps * nx * ny * nz * counts[0] * counts[1] * counts[2]
    hbm = pl.BlockSpec(memory_space=pltpu.HBM)
    vmem = pl.BlockSpec(memory_space=pltpu.VMEM)
    square = jax.ShapeDtypeStruct((vecs, vecs), F32)
    down = vecs // (nz // vecs)
    handed = pl.pallas_call(
        functools.partial(kernel, counts, dims),
        out_shape=(
            pltpu.VMEM(start.shape, F32),
            pltpu.VMEM((vecs, vecs), F32),
            pltpu.VMEM((vecs, vecs), F32),
        ),
        in_specs=[hbm, hbm, hbm],
        out_specs=(vmem, vmem, vmem),
        scratch_shapes=[
            pltpu.SMEM(lame.shape, F32),
            pltpu.VMEM(phase.shape, jnp.int32),
            pltpu.VMEM((steps + 1, comps, nx, vecs, ny, nz), F32),
            pltpu.VMEM((steps + 1, comps, 2, vecs, ny, nz), F32),
            pltpu.VMEM((steps, comps, 2, nx, vecs, nz), F32),
            pltpu.VMEM((steps + 1, comps, packs, ny, nz), F32),
            pltpu.VMEM((steps, comps, 2, packs, ny, nz), F32),
            pltpu.VMEM((phase.shape[0], ny, nz), F32),
            pltpu.VMEM((6, phase.shape[0], ny, nz), F32),
            pltpu.VMEM((comps, nx, 7, ny, nz), F32),
            pltpu.VMEM((comps, 2, tall, wide), BF16),
            pltpu.VMEM((2, tall, max(wide, tall)), BF16),
            pltpu.VMEM((2, tall, tall), F32),
            pltpu.VMEM((2, slots, down, nz), F32),
            pltpu.SemaphoreType.DMA((comps * nx + 2,)),
            pltpu.SemaphoreType.DMA((6,)),
            pltpu.SemaphoreType.DMA((6,)),
            pltpu.SemaphoreType.DMA((steps, comps, 6)),
            pltpu.SemaphoreType.DMA((steps, comps, 6)),
            pltpu.SemaphoreType.DMA((2, slots)),
            pltpu.SemaphoreType.DMA((2, slots)),
        ],
        compiler_params=pltpu.CompilerParams(
            collective_id=0, has_side_effects=True, vmem_limit_bytes=62 * 2**20
        ),
    )(lame, phase, start)
    handed = [pltpu.with_memory_space_constraint(one, pltpu.VMEM) for one in handed]
    return pl.pallas_call(
        functools.partial(finish, total_rows),
        out_shape=(jax.ShapeDtypeStruct(start.shape, F32), square),
        in_specs=[vmem, vmem, vmem],
        out_specs=(hbm, vmem),
        scratch_shapes=[pltpu.SemaphoreType.DMA],
        compiler_params=pltpu.CompilerParams(vmem_limit_bytes=4 * 2**20),
    )(*handed)


def solution(mesh):
    counts = tuple(mesh.shape[axis] for axis in AXES)
    spread = P(None, None, *AXES)
    return jax.shard_map(
        functools.partial(on_device, counts),
        mesh=mesh,
        in_specs=(P(*AXES), P(), spread),
        out_specs=(spread, P()),
        check_vma=False,
    )
```

```python
import functools

import jax
import jax.numpy as jnp
from jax import lax
from jax.experimental import pallas as pl
from jax.experimental.pallas import tpu as pltpu
from jax.sharding import PartitionSpec as P

ITERS = 3
PHASES = 2
BRICK = 4
LAG = 1
GROUP = 8
PANEL = 8
AXES = ("gx", "gy", "gz")
MESH = pl.DeviceIdType.MESH
F32 = jnp.float32
BF16 = jnp.bfloat16


def split(value, count):
    pieces = []
    for _ in range(count):
        piece = value.astype(BF16)
        pieces.append(piece)
        value = value - piece.astype(F32)
    return pieces


def contract_last(left, right):
    return lax.dot_general(
        left, right, (((1,), (1,)), ((), ())), preferred_element_type=F32
    )


def matmul(left, right):
    return jnp.dot(left, right, preferred_element_type=F32)


def inverse_factor(gram, size):
    row = lax.broadcasted_iota(jnp.int32, (size, size), 0)
    col = lax.broadcasted_iota(jnp.int32, (size, size), 1)
    both = jnp.concatenate([gram, jnp.where(row == col, 1.0, 0.0).astype(F32)], axis=1)
    rows = lax.broadcasted_iota(jnp.int32, both.shape, 0)
    for first in range(0, size, PANEL):
        columns = [
            jnp.broadcast_to(both[:, j : j + 1], both.shape)
            for j in range(first, first + PANEL)
        ]
        for t in range(PANEL):
            j = first + t
            scale = lax.rsqrt(columns[t][j : j + 1])
            column = columns[t] * scale
            pivot = both[j : j + 1] * scale
            below = jnp.where(rows > j, column, 0.0)
            both = jnp.where(rows == j, pivot, both - below * pivot)
            for u in range(t + 1, PANEL):
                columns[u] = columns[u] - column * column[first + u : first + u + 1]
    return both[:, size:]


def kernel(
    counts,
    dims,
    lame_in,
    phase_hbm,
    start,
    stage,
    mixing_out,
    form_out,
    lame,
    phase,
    field,
    plane_in,
    row_in,
    edge_out,
    edge_in,
    phase_near,
    weights,
    parts,
    image_parts,
    total_sum,
    sums,
    local_sem,
    phase_send,
    phase_recv,
    send_sem,
    recv_sem,
    sum_send,
    sum_recv,
):
    comps, vecs, nx, ny, nz = dims
    total_rows = 1.0 * comps * nx * ny * nz * counts[0] * counts[1] * counts[2]
    me = [lax.axis_index(axis) for axis in AXES]
    tall, wide = vecs * ny, nx * nz
    pairs = nz // 2
    packs = vecs * nx // pairs
    per = vecs // packs

    assert counts[0] - 1 <= ITERS
    everyone = counts[0] * counts[1] * counts[2]
    across = counts[1] * counts[2]
    place = (me[0] * counts[1] + me[1]) * counts[2] + me[2]

    def member(k):
        return {
            "gx": lax.div(k, across),
            "gy": lax.rem(lax.div(k, counts[2]), counts[1]),
            "gz": lax.rem(k, counts[2]),
        }

    barrier = pltpu.get_barrier_semaphore()

    def greet(device):
        pl.semaphore_signal(barrier, inc=1, device_id=device, device_id_type=MESH)

    def greet_line(step, _):
        greet({"gx": lax.rem(me[0] + step, counts[0])})
        return 0

    def greet_plane(step, _):
        k = lax.rem(me[1] * counts[2] + me[2] + step, across)
        greet({"gy": lax.div(k, counts[2]), "gz": lax.rem(k, counts[2])})
        return 0

    lax.fori_loop(1, counts[0], greet_line, 0)
    lax.fori_loop(1, across, greet_plane, 0)

    def each_other(action):
        def one(step, _):
            action(lax.rem(place + step, everyone))
            return 0

        lax.fori_loop(1, everyone, one, 0)

    small = [
        pltpu.make_async_copy(phase_hbm, phase, local_sem.at[comps * nx]),
        pltpu.make_async_copy(lame_in, lame, local_sem.at[comps * nx + 1]),
    ]
    for copy in small:
        copy.start()

    def load_copy(c, x):
        return pltpu.make_async_copy(
            start.at[c, :, x], field.at[0, c, x], local_sem.at[c * nx + x]
        )

    def load(k, _):
        load_copy(lax.div(k, nx), lax.rem(k, nx)).start()
        return 0

    lax.fori_loop(0, comps * nx, load, 0)

    def has(side):
        axis = side // 2
        return me[axis] > 0 if side % 2 == 0 else me[axis] < counts[axis] - 1

    def lacks(side):
        axis = side // 2
        return me[axis] == 0 if side % 2 == 0 else me[axis] == counts[axis] - 1

    def beside(side):
        axis = side // 2
        return {AXES[axis]: me[axis] - 1 if side % 2 == 0 else me[axis] + 1}

    def upward(c):
        return lax.rem(me[1] + c, 2) == 0

    def face(s, c, side, first=False):
        if side < 2:
            x = 0 if side == 0 else nx - 1
            src = start.at[c, :, x] if first else field.at[s, c, x]
            level = 0 if first else jnp.where(s == ITERS, ITERS + 1, s)
            dst = plane_in.at[level, c, 1 - side]
        elif side < 4:
            src = field.at[s, c, :, :, 0 if side == 2 else ny - 1]
            dst = row_in.at[s, c, 3 - side]
        else:
            src, dst = edge_out.at[s, c], edge_in.at[s, c, 5 - side]
        return src, dst

    def send_copy(s, c, side, first=False):
        src, dst = face(s, c, side, first)
        return pltpu.make_async_remote_copy(
            src_ref=src,
            dst_ref=dst,
            send_sem=send_sem.at[s, c, side],
            recv_sem=recv_sem.at[s, c, side ^ 1],
            device_id=beside(side),
            device_id_type=MESH,
        )

    def recv_copy(s, c, side):
        src, dst = face(s, c, side ^ 1)
        return pltpu.make_async_remote_copy(
            src_ref=src,
            dst_ref=dst,
            send_sem=send_sem.at[s, c, side],
            recv_sem=recv_sem.at[s, c, side],
            device_id=beside(side),
            device_id_type=MESH,
        )

    def sends(s, c, side):
        if side >= 2:
            return has(side)
        way = upward(c) if side == 1 else jnp.logical_not(upward(c))
        return has(side) & ((s < ITERS) | way)

    def send(s, c, sides, first=False):
        for side in sides:

            @pl.when(has(side) if first else sends(s, c, side))
            def _(side=side):
                send_copy(s, c, side, first).start()

    def receive(s, c, sides):
        for side in sides:

            @pl.when(has(side))
            def _(side=side):
                recv_copy(s, c, side).wait_recv()

    def phase_copy(side, signal):
        return pltpu.make_async_remote_copy(
            src_ref=phase_hbm,
            dst_ref=phase_near.at[signal],
            send_sem=phase_send.at[side],
            recv_sem=phase_recv.at[signal],
            device_id=beside(side),
            device_id_type=MESH,
        )

    lane = lax.broadcasted_iota(jnp.int32, (ny, nz), 1)
    line = lax.broadcasted_iota(jnp.int32, (ny, nz), 0)
    pair = lax.rem(lax.div(lane + 1, 2), pairs)

    turned = lax.rem(lane + 1, nz)

    def side_by_side(values, width):
        total = None
        for k, value in enumerate(values):
            if total is None:
                total = value
            else:
                moved = pltpu.roll(value, k * width, 1)
                total = jnp.where(turned < k * width, total, moved)
        return total

    def edges_of(s, c):
        for e in range(packs):
            blocks = []
            for first in range(0, pairs, GROUP):
                values = []
                for m in range(first, first + GROUP):
                    values.append(field[s, c, m % nx, e * per + m // nx])
                blocks.append(side_by_side(values, 2))
            edge_out[s, c, e] = side_by_side(blocks, 2 * GROUP)

    pl.semaphore_wait(barrier, counts[0] + across - 2)

    for side in range(6):

        @pl.when(has(side))
        def _(side=side):
            phase_copy(side, side ^ 1).start()

    def first_planes(c, _):
        send(0, c, range(2), True)
        return 0

    lax.fori_loop(0, comps, first_planes, 0)
    def first_edges(c, _):
        for x in range(nx):
            load_copy(c, x).wait()
        send(0, c, range(2, 4))

        edges_of(0, c)
        send(0, c, range(4, 6))
        return 0

    lax.fori_loop(0, comps, first_edges, 0)

    plane = jnp.zeros((ny, nz), F32)
    for side in range(2):

        def leave_out(v, _, side=side):
            for c in range(comps):
                plane_in[ITERS, c, side, v] = plane
            return 0

        lax.fori_loop(0, vecs, leave_out, 0)

        @pl.when(lacks(side))
        def _(side=side):
            def clear(v, _):
                for s in range(ITERS):
                    for c in range(comps):
                        plane_in[s, c, side, v] = plane
                return 0

            lax.fori_loop(0, vecs, clear, 0)

        @pl.when(lacks(2 + side))
        def _(side=side):
            def clear(k, _):
                s, c = lax.div(k, comps), lax.rem(k, comps)
                row_in[s, c, side] = jnp.zeros((nx, vecs, nz), F32)
                return 0

            lax.fori_loop(0, (ITERS + 1) * comps, clear, 0)

        @pl.when(lacks(4 + side))
        def _(side=side):
            def clear(k, _):
                s, c = lax.div(k, comps), lax.rem(k, comps)
                edge_in[s, c, side] = jnp.zeros((packs, ny, nz), F32)
                return 0

            lax.fori_loop(0, (ITERS + 1) * comps, clear, 0)

    for side in range(6):

        @pl.when(lacks(side))
        def _(side=side):
            phase_near[side] = jnp.zeros(phase_near.shape[1:], jnp.int32)

    for side in range(6):

        @pl.when(has(side))
        def _(side=side):
            phase_copy(side, side).wait_recv()

    for copy in small:
        copy.wait()
    bricks_x, bricks_y, bricks_z = phase.shape
    spread = jnp.where(
        lax.broadcasted_iota(jnp.int32, (bricks_z, nz), 1) // BRICK
        == lax.broadcasted_iota(jnp.int32, (bricks_z, nz), 0),
        1.0,
        0.0,
    ).astype(F32)
    row_brick = lax.broadcasted_iota(jnp.int32, (ny, bricks_z), 0) // BRICK
    tiles = []
    for block in [phase] + [phase_near.at[side] for side in range(6)]:
        for bx in range(bricks_x):
            bricks = block[bx].astype(F32)
            rows = jnp.zeros((ny, bricks_z), F32)
            for by in range(bricks_y):
                one = jnp.broadcast_to(bricks[by : by + 1], (ny, bricks_z))
                rows = jnp.where(row_brick == by, one, rows)
            tiles.append(rows)
    kinds = jnp.dot(
        jnp.concatenate(tiles, axis=0), spread, preferred_element_type=F32
    )

    def kind(block, bx):
        at = (block * bricks_x + bx) * ny
        return kinds[at : at + ny]

    def material(own):
        shear = jnp.zeros(own.shape, F32)
        first = jnp.zeros(own.shape, F32)
        for index in range(PHASES):
            hit = own == float(index)
            shear = shear + jnp.where(hit, lame[index, 0], 0.0)
            first = first + jnp.where(hit, lame[index, 1], 0.0)
        return shear, first + shear

    for x in range(nx):
        bx = x // BRICK
        own = kind(0, bx)
        others = [
            kind(0, (x - 1) // BRICK) if x > 0 else kind(1, bricks_x - 1),
            kind(0, (x + 1) // BRICK) if x < nx - 1 else kind(2, 0),
            pltpu.roll(jnp.where(line == ny - 1, kind(3, bx), own), 1, 0),
            pltpu.roll(jnp.where(line == 0, kind(4, bx), own), ny - 1, 0),
            pltpu.roll(jnp.where(lane == nz - 1, kind(5, bx), own), 1, 1),
            pltpu.roll(jnp.where(lane == 0, kind(6, bx), own), nz - 1, 1),
        ]
        shear_c, grow_c = material(own)
        total = [None] * comps
        for side in range(6):
            shear_n, grow_n = material(others[side])
            w_shear = 0.5 * (shear_c + shear_n)
            w_grow = 0.5 * (grow_c + grow_n)
            for c in range(comps):
                w = w_shear + w_grow if side // 2 == c else w_shear
                weights[c, x, side] = w
                total[c] = w if total[c] is None else total[c] + w
        for c in range(comps):
            weights[c, x, 6] = total[c]

    def image(s, c, v, edges, at):
        value = [plane_in[s, c, 0, v]]
        value += [field[s, c, x, v] for x in range(nx)]
        value += [plane_in[s, c, 1, v]]
        totals = []
        for x in range(nx):
            centre = value[x + 1]
            shift = 2 * (at * nx + x)
            border = pltpu.roll(edges, nz - shift, 1) if shift else edges
            low = jnp.broadcast_to(row_in[s, c, 0, x, pl.ds(v, 1), :], (ny, nz))
            high = jnp.broadcast_to(row_in[s, c, 1, x, pl.ds(v, 1), :], (ny, nz))
            others = [
                value[x],
                value[x + 2],
                jnp.where(line == 0, low, pltpu.roll(centre, 1, 0)),
                jnp.where(line == ny - 1, high, pltpu.roll(centre, ny - 1, 0)),
                jnp.where(lane == 0, border, pltpu.roll(centre, 1, 1)),
                jnp.where(lane == nz - 1, border, pltpu.roll(centre, nz - 1, 1)),
            ]
            total = weights[c, x, 6] * centre
            for side in range(6):
                total = total - weights[c, x, side] * others[side]
            totals.append(total)
        return totals

    def apply(s, c):
        def step(e, _):
            edges = jnp.where(
                lax.rem(lane, 2) == 0,
                pltpu.roll(edge_in[s, c, 0, e], 1, 1),
                pltpu.roll(edge_in[s, c, 1, e], nz - 1, 1),
            )
            for at in range(per):
                v = e * per + at
                out = image(s, c, v, edges, at)
                for x in range(nx):
                    field[s + 1, c, x, v] = out[x]
            return 0

        lax.fori_loop(0, packs, step, 0)

    def put_parts(s, c, ref):
        for x in range(nx):
            high, low = split(field[s, c, x].reshape(tall, nz), 2)
            ref[0, :, x * nz : (x + 1) * nz] = high
            ref[1, :, x * nz : (x + 1) * nz] = low

    def sum_copy(which, slot, other):
        return pltpu.make_async_remote_copy(
            src_ref=sums.at[which, slot],
            dst_ref=sums.at[which, slot],
            send_sem=sum_send.at[which, other],
            recv_sem=sum_recv.at[which, slot],
            device_id=member(other),
            device_id_type=MESH,
        )

    def sum_start(which, value):
        sums[which, place] = value
        each_other(lambda k: sum_copy(which, place, k).start())

    def sum_end(which):
        each_other(lambda k: sum_copy(which, k, k).wait_recv())
        total = sums[which, 0]
        for k in range(1, everyone):
            total = total + sums[which, k]
        return total

    down_n = sums.shape[2]
    across_n = vecs // down_n

    def fold(acc):
        keep = (
            lax.broadcasted_iota(jnp.int32, (vecs, ny, tall), 1)
            == lax.broadcasted_iota(jnp.int32, (vecs, ny, tall), 2) % ny
        )
        rows = jnp.sum(jnp.where(keep, acc.reshape(vecs, ny, tall), 0.0), axis=1)
        flat = jnp.concatenate(
            [rows[k * down_n : (k + 1) * down_n] for k in range(across_n)], axis=1
        )
        pieces = jnp.concatenate([p.astype(F32) for p in split(flat, 3)], axis=0)
        source = lax.broadcasted_iota(jnp.int32, (across_n * tall, across_n * vecs), 0)
        target = lax.broadcasted_iota(jnp.int32, (across_n * tall, across_n * vecs), 1)
        to = jnp.where(source // ny == target, 1.0, 0.0).astype(BF16)
        out = matmul(pieces.astype(BF16), to)
        return out[:down_n] + out[down_n : 2 * down_n] + out[2 * down_n :]

    def unpacked(value):
        pieces = [value[:, k * vecs : (k + 1) * vecs] for k in range(across_n)]
        square = jnp.concatenate(pieces, axis=0)
        return 0.5 * (square + square.T)

    def advance(s, c):
        receive(s, c, range(6))
        apply(s, c)
        send(s + 1, c, range(4))
        edges_of(s + 1, c)
        send(s + 1, c, range(4, 6))

    def early(k, _):
        advance(lax.div(k, comps), lax.rem(k, comps))
        return 0

    def gram_of(c):
        put_parts(ITERS, c, parts.at[c])
        side = contract_last(parts[c, 0], parts[c, 1])
        total_sum[0] += contract_last(parts[c, 0], parts[c, 0]) + (side + side)

    def form_of(c):
        receive(ITERS, c, range(2, 6))
        apply(ITERS, c)
        put_parts(ITERS + 1, c, image_parts)
        more = contract_last(parts[c, 0], image_parts[0])
        more = more + contract_last(parts[c, 1], image_parts[0])
        total_sum[1] += more + contract_last(parts[c, 0], image_parts[1])

    lax.fori_loop(0, (ITERS - 1) * comps, early, 0)
    total_sum[...] = jnp.zeros(total_sum.shape, F32)

    def last(k, _):
        @pl.when(k < comps)
        def _():
            advance(ITERS - 1, k)
            gram_of(k)

        @pl.when(k == comps - 1)
        def _():
            sum_start(0, fold(total_sum[0]))

        @pl.when(k >= LAG)
        def _():
            form_of(k - LAG)

        return 0

    lax.fori_loop(0, comps + LAG, last, 0)
    def cut(c, _):
        way = upward(c)
        side = jnp.where(way, 0, 1)
        x = jnp.where(way, 0, nx - 1)

        @pl.when(jnp.where(way, me[0], counts[0] - 1 - me[0]) > 0)
        def _():
            pltpu.make_async_remote_copy(
                src_ref=field.at[ITERS, c, 0],
                dst_ref=plane_in.at[ITERS + 1, c, side],
                send_sem=send_sem.at[ITERS, c, side],
                recv_sem=recv_sem.at[ITERS, c, side],
                device_id={"gx": me[0] + 1 - 2 * jnp.where(way, 1, 0)},
                device_id_type=MESH,
            ).wait_recv()
            there = plane_in[ITERS + 1, c, side] * (-2.0 * weights[c, x, side])
            high, low = split(there.reshape(tall, nz), 2)
            here = pl.ds(pl.multiple_of(x * nz, nz), nz)
            own = [parts[c, p, :, here] for p in range(2)]
            more = contract_last(own[0], high) + contract_last(own[1], high)
            total_sum[1] += more + contract_last(own[0], low)

        return 0

    lax.fori_loop(0, comps, cut, 0)
    sum_start(1, fold(total_sum[1]))
    gram = sum_end(0)
    mixing = inverse_factor(unpacked(gram) / total_rows, vecs)
    mixing_out[...] = mixing

    widen = jnp.where(
        lax.broadcasted_iota(jnp.int32, (vecs, tall), 0)
        == lax.broadcasted_iota(jnp.int32, (vecs, tall), 1) // ny,
        1.0,
        0.0,
    ).astype(BF16)
    same = (
        lax.broadcasted_iota(jnp.int32, (tall, tall), 0) % ny
        == lax.broadcasted_iota(jnp.int32, (tall, tall), 1) % ny
    )
    mixers = []
    for piece in split(mixing, 2):
        tallest = jnp.broadcast_to(piece.astype(F32)[:, None, :], (vecs, ny, vecs))
        big = matmul(tallest.reshape(tall, vecs).astype(BF16), widen)
        mixers.append(jnp.where(same, big, 0.0).astype(BF16))
    for p in range(2):
        image_parts[p, :, :tall] = mixers[p]

    def mix(c, _):
        for x in range(0, nx, 2):
            high, low = (parts[c, p, :, x * nz : (x + 2) * nz] for p in range(2))
            left = [image_parts[p, :, :tall] for p in range(2)]
            out = matmul(left[0], high) + matmul(left[1], high)
            out = out + matmul(left[0], low)
            for t in range(2):
                stage[c, :, x + t] = out[:, t * nz : (t + 1) * nz].reshape(vecs, ny, nz)
        return 0

    lax.fori_loop(0, comps, mix, 0)
    form_out[...] = unpacked(sum_end(1))

    def sent(k, _):
        s, c = lax.div(k, comps), lax.rem(k, comps)
        for side in range(6):

            @pl.when(sends(s, c, side))
            def _(side=side):
                send_copy(s, c, side).wait_send()

        return 0

    lax.fori_loop(0, (ITERS + 1) * comps, sent, 0)
    for side in range(6):

        @pl.when(has(side))
        def _(side=side):
            phase_copy(side, side ^ 1).wait_send()

    for which in range(2):
        each_other(lambda k: sum_copy(which, place, k).wait_send())


def finish(total_rows, stage, mixing, form, basis, coarse, small, sem):
    copy = pltpu.make_async_copy(stage, basis, sem.at[0])
    copy.start()
    exact = lax.Precision.HIGHEST
    left = mixing[...]
    first = jnp.dot(left, form[...], precision=exact, preferred_element_type=F32)
    small[...] = (
        lax.dot_general(
            first,
            left,
            (((1,), (1,)), ((), ())),
            precision=exact,
            preferred_element_type=F32,
        )
        / total_rows
    )
    other = pltpu.make_async_copy(small, coarse, sem.at[1])
    other.start()
    other.wait()
    copy.wait()


def on_device(counts, phase, lame, start):
    comps, vecs, nx, ny, nz = dims = start.shape
    packs = 2 * vecs * nx // nz
    tall, wide = vecs * ny, nx * nz
    assert comps == 3 and nx % 2 == 0 and ny == 8 and nz % 128 == 0
    assert (nz // 2) % GROUP == 0 and vecs % PANEL == 0
    assert packs * nz == 2 * vecs * nx and vecs % (2 * packs) == 0
    slots = counts[0] * counts[1] * counts[2]
    steps = ITERS + 1
    total_rows = 1.0 * comps * nx * ny * nz * counts[0] * counts[1] * counts[2]
    hbm = pl.BlockSpec(memory_space=pltpu.HBM)
    vmem = pl.BlockSpec(memory_space=pltpu.VMEM)
    square = jax.ShapeDtypeStruct((vecs, vecs), F32)
    down = vecs // (nz // vecs)
    handed = pl.pallas_call(
        functools.partial(kernel, counts, dims),
        out_shape=(
            pltpu.VMEM(start.shape, F32),
            pltpu.VMEM((vecs, vecs), F32),
            pltpu.VMEM((vecs, vecs), F32),
        ),
        in_specs=[hbm, hbm, hbm],
        out_specs=(vmem, vmem, vmem),
        scratch_shapes=[
            pltpu.SMEM(lame.shape, F32),
            pltpu.VMEM(phase.shape, jnp.int32),
            pltpu.VMEM((steps + 1, comps, nx, vecs, ny, nz), F32),
            pltpu.VMEM((steps + 1, comps, 2, vecs, ny, nz), F32),
            pltpu.VMEM((steps, comps, 2, nx, vecs, nz), F32),
            pltpu.VMEM((steps + 1, comps, packs, ny, nz), F32),
            pltpu.VMEM((steps, comps, 2, packs, ny, nz), F32),
            pltpu.VMEM((6,) + phase.shape, jnp.int32),
            pltpu.VMEM((comps, nx, 7, ny, nz), F32),
            pltpu.VMEM((comps, 2, tall, wide), BF16),
            pltpu.VMEM((2, tall, max(wide, tall)), BF16),
            pltpu.VMEM((2, tall, tall), F32),
            pltpu.VMEM((2, slots, down, nz), F32),
            pltpu.SemaphoreType.DMA((comps * nx + 2,)),
            pltpu.SemaphoreType.DMA((6,)),
            pltpu.SemaphoreType.DMA((6,)),
            pltpu.SemaphoreType.DMA((steps, comps, 6)),
            pltpu.SemaphoreType.DMA((steps, comps, 6)),
            pltpu.SemaphoreType.DMA((2, slots)),
            pltpu.SemaphoreType.DMA((2, slots)),
        ],
        compiler_params=pltpu.CompilerParams(
            collective_id=0, has_side_effects=True, vmem_limit_bytes=62 * 2**20
        ),
    )(lame, phase, start)
    handed = [pltpu.with_memory_space_constraint(one, pltpu.VMEM) for one in handed]
    return pl.pallas_call(
        functools.partial(finish, total_rows),
        out_shape=(jax.ShapeDtypeStruct(start.shape, F32), square),
        in_specs=[vmem, vmem, vmem],
        out_specs=(hbm, hbm),
        scratch_shapes=[
            pltpu.VMEM((vecs, vecs), F32),
            pltpu.SemaphoreType.DMA((2,)),
        ],
        compiler_params=pltpu.CompilerParams(vmem_limit_bytes=4 * 2**20),
    )(*handed)


def solution(mesh):
    counts = tuple(mesh.shape[axis] for axis in AXES)
    spread = P(None, None, *AXES)
    return jax.shard_map(
        functools.partial(on_device, counts),
        mesh=mesh,
        in_specs=(P(*AXES), P(), spread),
        out_specs=(spread, P()),
        check_vma=False,
    )
```

```python
import functools

import jax
import jax.numpy as jnp
from jax import lax
from jax.experimental import pallas as pl
from jax.experimental.pallas import tpu as pltpu
from jax.sharding import PartitionSpec as P

ITERS = 3
PHASES = 2
BRICK = 4
LAG = 1
GROUP = 8
PANEL = 8
AXES = ("gx", "gy", "gz")
MESH = pl.DeviceIdType.MESH
F32 = jnp.float32
BF16 = jnp.bfloat16


def split(value, count):
    pieces = []
    for _ in range(count):
        piece = value.astype(BF16)
        pieces.append(piece)
        value = value - piece.astype(F32)
    return pieces


def contract_last(left, right):
    return lax.dot_general(
        left, right, (((1,), (1,)), ((), ())), preferred_element_type=F32
    )


def matmul(left, right):
    return jnp.dot(left, right, preferred_element_type=F32)


def inverse_factor(gram, size):
    row = lax.broadcasted_iota(jnp.int32, (size, size), 0)
    col = lax.broadcasted_iota(jnp.int32, (size, size), 1)
    both = jnp.concatenate([gram, jnp.where(row == col, 1.0, 0.0).astype(F32)], axis=1)
    rows = lax.broadcasted_iota(jnp.int32, both.shape, 0)
    for first in range(0, size, PANEL):
        columns = [
            jnp.broadcast_to(both[:, j : j + 1], both.shape)
            for j in range(first, first + PANEL)
        ]
        for t in range(PANEL):
            j = first + t
            scale = lax.rsqrt(columns[t][j : j + 1])
            column = columns[t] * scale
            pivot = both[j : j + 1] * scale
            below = jnp.where(rows > j, column, 0.0)
            both = jnp.where(rows == j, pivot, both - below * pivot)
            for u in range(t + 1, PANEL):
                columns[u] = columns[u] - column * column[first + u : first + u + 1]
    return both[:, size:]


def kernel(
    counts,
    dims,
    lame_in,
    phase_hbm,
    start,
    stage,
    mixing_out,
    form_out,
    lame,
    phase,
    field,
    plane_in,
    row_in,
    edge_out,
    edge_in,
    phase_near,
    weights,
    parts,
    image_parts,
    total_sum,
    sums,
    local_sem,
    phase_send,
    phase_recv,
    send_sem,
    recv_sem,
    sum_send,
    sum_recv,
):
    comps, vecs, nx, ny, nz = dims
    total_rows = 1.0 * comps * nx * ny * nz * counts[0] * counts[1] * counts[2]
    me = [lax.axis_index(axis) for axis in AXES]
    tall, wide = vecs * ny, nx * nz
    pairs = nz // 2
    packs = vecs * nx // pairs
    per = vecs // packs

    assert counts[0] - 1 <= ITERS
    everyone = counts[0] * counts[1] * counts[2]
    across = counts[1] * counts[2]

    def slot_of(device):
        return (device[0] * counts[1] + device[1]) * counts[2] + device[2]

    place = slot_of(me)
    turns = [
        [lax.rem(me[axis] + step, counts[axis]) for step in range(counts[axis])]
        for axis in (1, 2)
    ]

    def has(side):
        axis = side // 2
        return me[axis] > 0 if side % 2 == 0 else me[axis] < counts[axis] - 1

    def beside(side):
        axis = side // 2
        return {AXES[axis]: me[axis] - 1 if side % 2 == 0 else me[axis] + 1}

    barrier = pltpu.get_barrier_semaphore()

    def greet(device):
        pl.semaphore_signal(barrier, inc=1, device_id=device, device_id_type=MESH)

    def greet_plane(step, _):
        k = lax.rem(me[1] * counts[2] + me[2] + step, across)
        greet({"gy": lax.div(k, counts[2]), "gz": lax.rem(k, counts[2])})
        return 0

    for side in range(2):

        @pl.when(has(side))
        def _(side=side):
            greet(beside(side))

    lax.fori_loop(1, across, greet_plane, 0)

    def each_other(action):
        def plane(step, own):
            gx = lax.rem(me[0] + step, counts[0])
            for y, gy in enumerate(turns[0]):
                for z, gz in enumerate(turns[1]):
                    if y + z > 0 or not own:
                        action((gx, gy, gz))

        def one(step, _):
            plane(step, False)
            return 0

        lax.fori_loop(1, counts[0], one, 0)
        plane(0, True)

    def lacks(side):
        axis = side // 2
        return me[axis] == 0 if side % 2 == 0 else me[axis] == counts[axis] - 1

    def upward(c):
        return lax.rem(me[1] + c, 2) == 0

    def face(s, c, side, first=False):
        if side < 2:
            x = 0 if side == 0 else nx - 1
            src = start.at[c, :, x] if first else field.at[s, c, x]
            level = 0 if first else jnp.where(s == ITERS, ITERS + 1, s)
            dst = plane_in.at[level, c, 1 - side]
        elif side < 4:
            src = field.at[s, c, :, :, 0 if side == 2 else ny - 1]
            dst = row_in.at[s, c, 3 - side]
        else:
            src, dst = edge_out.at[s, c], edge_in.at[s, c, 5 - side]
        return src, dst

    def send_copy(s, c, side, first=False):
        src, dst = face(s, c, side, first)
        return pltpu.make_async_remote_copy(
            src_ref=src,
            dst_ref=dst,
            send_sem=send_sem.at[s, c, side],
            recv_sem=recv_sem.at[s, c, side ^ 1],
            device_id=beside(side),
            device_id_type=MESH,
        )

    def recv_copy(s, c, side):
        src, dst = face(s, c, side ^ 1)
        return pltpu.make_async_remote_copy(
            src_ref=src,
            dst_ref=dst,
            send_sem=send_sem.at[s, c, side],
            recv_sem=recv_sem.at[s, c, side],
            device_id=beside(side),
            device_id_type=MESH,
        )

    def sends(s, c, side):
        if side >= 2:
            return has(side)
        way = upward(c) if side == 1 else jnp.logical_not(upward(c))
        return has(side) & ((s < ITERS) | way)

    def send(s, c, sides, first=False):
        for side in sides:

            @pl.when(has(side) if first else sends(s, c, side))
            def _(side=side):
                send_copy(s, c, side, first).start()

    def receive(s, c, sides):
        for side in sides:

            @pl.when(has(side))
            def _(side=side):
                recv_copy(s, c, side).wait_recv()

    def phase_copy(side, signal):
        return pltpu.make_async_remote_copy(
            src_ref=phase_hbm,
            dst_ref=phase_near.at[signal],
            send_sem=phase_send.at[side],
            recv_sem=phase_recv.at[signal],
            device_id=beside(side),
            device_id_type=MESH,
        )

    lane = lax.broadcasted_iota(jnp.int32, (ny, nz), 1)
    line = lax.broadcasted_iota(jnp.int32, (ny, nz), 0)
    pair = lax.rem(lax.div(lane + 1, 2), pairs)

    turned = lax.rem(lane + 1, nz)

    def side_by_side(values, width):
        total = None
        for k, value in enumerate(values):
            if total is None:
                total = value
            else:
                moved = pltpu.roll(value, k * width, 1)
                total = jnp.where(turned < k * width, total, moved)
        return total

    def edges_of(s, c):
        for e in range(packs):
            blocks = []
            for first in range(0, pairs, GROUP):
                values = []
                for m in range(first, first + GROUP):
                    values.append(field[s, c, m % nx, e * per + m // nx])
                blocks.append(side_by_side(values, 2))
            edge_out[s, c, e] = side_by_side(blocks, 2 * GROUP)

    near = jnp.where(has(0), 1, 0) + jnp.where(has(1), 1, 0)
    pl.semaphore_wait(barrier, near + across - 1)

    for side in range(6):

        @pl.when(has(side))
        def _(side=side):
            phase_copy(side, side ^ 1).start()

    def first_planes(c, _):
        send(0, c, range(2), True)
        return 0

    lax.fori_loop(0, comps, first_planes, 0)

    small = [
        pltpu.make_async_copy(phase_hbm, phase, local_sem.at[comps * nx]),
        pltpu.make_async_copy(lame_in, lame, local_sem.at[comps * nx + 1]),
    ]
    for copy in small:
        copy.start()

    def load_copy(c, x):
        return pltpu.make_async_copy(
            start.at[c, :, x], field.at[0, c, x], local_sem.at[c * nx + x]
        )

    def load(k, _):
        load_copy(lax.div(k, nx), lax.rem(k, nx)).start()
        return 0

    lax.fori_loop(0, comps * nx, load, 0)
    def first_edges(c, _):
        for x in range(nx):
            load_copy(c, x).wait()
        send(0, c, range(2, 4))

        edges_of(0, c)
        send(0, c, range(4, 6))
        return 0

    lax.fori_loop(0, comps, first_edges, 0)

    plane = jnp.zeros((ny, nz), F32)
    for side in range(2):

        def leave_out(v, _, side=side):
            for c in range(comps):
                plane_in[ITERS, c, side, v] = plane
            return 0

        lax.fori_loop(0, vecs, leave_out, 0)

        @pl.when(lacks(side))
        def _(side=side):
            def clear(v, _):
                for s in range(ITERS):
                    for c in range(comps):
                        plane_in[s, c, side, v] = plane
                return 0

            lax.fori_loop(0, vecs, clear, 0)

        @pl.when(lacks(2 + side))
        def _(side=side):
            def clear(k, _):
                s, c = lax.div(k, comps), lax.rem(k, comps)
                row_in[s, c, side] = jnp.zeros((nx, vecs, nz), F32)
                return 0

            lax.fori_loop(0, (ITERS + 1) * comps, clear, 0)

        @pl.when(lacks(4 + side))
        def _(side=side):
            def clear(k, _):
                s, c = lax.div(k, comps), lax.rem(k, comps)
                edge_in[s, c, side] = jnp.zeros((packs, ny, nz), F32)
                return 0

            lax.fori_loop(0, (ITERS + 1) * comps, clear, 0)

    for side in range(6):

        @pl.when(lacks(side))
        def _(side=side):
            phase_near[side] = jnp.zeros(phase_near.shape[1:], jnp.int32)

    for side in range(6):

        @pl.when(has(side))
        def _(side=side):
            phase_copy(side, side).wait_recv()

    for copy in small:
        copy.wait()
    bricks_x, bricks_y, bricks_z = phase.shape
    spread = jnp.where(
        lax.broadcasted_iota(jnp.int32, (bricks_z, nz), 1) // BRICK
        == lax.broadcasted_iota(jnp.int32, (bricks_z, nz), 0),
        1.0,
        0.0,
    ).astype(F32)
    row_brick = lax.broadcasted_iota(jnp.int32, (ny, bricks_z), 0) // BRICK
    tiles = []
    for block in [phase] + [phase_near.at[side] for side in range(6)]:
        for bx in range(bricks_x):
            bricks = block[bx].astype(F32)
            rows = jnp.zeros((ny, bricks_z), F32)
            for by in range(bricks_y):
                one = jnp.broadcast_to(bricks[by : by + 1], (ny, bricks_z))
                rows = jnp.where(row_brick == by, one, rows)
            tiles.append(rows)
    kinds = jnp.dot(
        jnp.concatenate(tiles, axis=0), spread, preferred_element_type=F32
    )

    def kind(block, bx):
        at = (block * bricks_x + bx) * ny
        return kinds[at : at + ny]

    def material(own):
        shear = jnp.zeros(own.shape, F32)
        first = jnp.zeros(own.shape, F32)
        for index in range(PHASES):
            hit = own == float(index)
            shear = shear + jnp.where(hit, lame[index, 0], 0.0)
            first = first + jnp.where(hit, lame[index, 1], 0.0)
        return shear, first + shear

    for x in range(nx):
        bx = x // BRICK
        own = kind(0, bx)
        others = [
            kind(0, (x - 1) // BRICK) if x > 0 else kind(1, bricks_x - 1),
            kind(0, (x + 1) // BRICK) if x < nx - 1 else kind(2, 0),
            pltpu.roll(jnp.where(line == ny - 1, kind(3, bx), own), 1, 0),
            pltpu.roll(jnp.where(line == 0, kind(4, bx), own), ny - 1, 0),
            pltpu.roll(jnp.where(lane == nz - 1, kind(5, bx), own), 1, 1),
            pltpu.roll(jnp.where(lane == 0, kind(6, bx), own), nz - 1, 1),
        ]
        shear_c, grow_c = material(own)
        total = [None] * comps
        for side in range(6):
            shear_n, grow_n = material(others[side])
            w_shear = 0.5 * (shear_c + shear_n)
            w_grow = 0.5 * (grow_c + grow_n)
            for c in range(comps):
                w = w_shear + w_grow if side // 2 == c else w_shear
                weights[c, x, side] = w
                total[c] = w if total[c] is None else total[c] + w
        for c in range(comps):
            weights[c, x, 6] = total[c]

    def image(s, c, v, edges, at):
        value = [plane_in[s, c, 0, v]]
        value += [field[s, c, x, v] for x in range(nx)]
        value += [plane_in[s, c, 1, v]]
        totals = []
        for x in range(nx):
            centre = value[x + 1]
            shift = 2 * (at * nx + x)
            border = pltpu.roll(edges, nz - shift, 1) if shift else edges
            low = jnp.broadcast_to(row_in[s, c, 0, x, pl.ds(v, 1), :], (ny, nz))
            high = jnp.broadcast_to(row_in[s, c, 1, x, pl.ds(v, 1), :], (ny, nz))
            others = [
                value[x],
                value[x + 2],
                jnp.where(line == 0, low, pltpu.roll(centre, 1, 0)),
                jnp.where(line == ny - 1, high, pltpu.roll(centre, ny - 1, 0)),
                jnp.where(lane == 0, border, pltpu.roll(centre, 1, 1)),
                jnp.where(lane == nz - 1, border, pltpu.roll(centre, nz - 1, 1)),
            ]
            total = weights[c, x, 6] * centre
            for side in range(6):
                total = total - weights[c, x, side] * others[side]
            totals.append(total)
        return totals

    def apply(s, c):
        def step(e, _):
            edges = jnp.where(
                lax.rem(lane, 2) == 0,
                pltpu.roll(edge_in[s, c, 0, e], 1, 1),
                pltpu.roll(edge_in[s, c, 1, e], nz - 1, 1),
            )
            for at in range(per):
                v = e * per + at
                out = image(s, c, v, edges, at)
                for x in range(nx):
                    field[s + 1, c, x, v] = out[x]
            return 0

        lax.fori_loop(0, packs, step, 0)

    def put_parts(s, c, ref):
        for x in range(nx):
            high, low = split(field[s, c, x].reshape(tall, nz), 2)
            ref[0, :, x * nz : (x + 1) * nz] = high
            ref[1, :, x * nz : (x + 1) * nz] = low

    def sum_copy(which, source, target):
        slot = slot_of(source)
        return pltpu.make_async_remote_copy(
            src_ref=sums.at[which, slot],
            dst_ref=sums.at[which, slot],
            send_sem=sum_send.at[which, slot_of(target)],
            recv_sem=sum_recv.at[which, slot],
            device_id=dict(zip(AXES, target)),
            device_id_type=MESH,
        )

    def sum_start(which, value):
        sums[which, place] = value
        each_other(lambda other: sum_copy(which, me, other).start())

    def sum_end(which):
        each_other(lambda other: sum_copy(which, other, other).wait_recv())
        total = sums[which, 0]
        for k in range(1, everyone):
            total = total + sums[which, k]
        return total

    down_n = sums.shape[2]
    across_n = vecs // down_n

    def fold(acc):
        keep = (
            lax.broadcasted_iota(jnp.int32, (vecs, ny, tall), 1)
            == lax.broadcasted_iota(jnp.int32, (vecs, ny, tall), 2) % ny
        )
        rows = jnp.sum(jnp.where(keep, acc.reshape(vecs, ny, tall), 0.0), axis=1)
        flat = jnp.concatenate(
            [rows[k * down_n : (k + 1) * down_n] for k in range(across_n)], axis=1
        )
        pieces = jnp.concatenate([p.astype(F32) for p in split(flat, 3)], axis=0)
        source = lax.broadcasted_iota(jnp.int32, (across_n * tall, across_n * vecs), 0)
        target = lax.broadcasted_iota(jnp.int32, (across_n * tall, across_n * vecs), 1)
        to = jnp.where(source // ny == target, 1.0, 0.0).astype(BF16)
        out = matmul(pieces.astype(BF16), to)
        return out[:down_n] + out[down_n : 2 * down_n] + out[2 * down_n :]

    def unpacked(value):
        pieces = [value[:, k * vecs : (k + 1) * vecs] for k in range(across_n)]
        square = jnp.concatenate(pieces, axis=0)
        return 0.5 * (square + square.T)

    def advance(s, c):
        receive(s, c, range(6))
        apply(s, c)
        send(s + 1, c, range(4))
        edges_of(s + 1, c)
        send(s + 1, c, range(4, 6))

    def early(k, _):
        advance(lax.div(k, comps), lax.rem(k, comps))
        return 0

    def gram_of(c):
        put_parts(ITERS, c, parts.at[c])
        side = contract_last(parts[c, 0], parts[c, 1])
        total_sum[0] += contract_last(parts[c, 0], parts[c, 0]) + (side + side)

    def form_of(c):
        receive(ITERS, c, range(2, 6))
        apply(ITERS, c)
        put_parts(ITERS + 1, c, image_parts)
        more = contract_last(parts[c, 0], image_parts[0])
        more = more + contract_last(parts[c, 1], image_parts[0])
        total_sum[1] += more + contract_last(parts[c, 0], image_parts[1])

    lax.fori_loop(0, (ITERS - 1) * comps, early, 0)
    total_sum[...] = jnp.zeros(total_sum.shape, F32)

    def last(k, _):
        @pl.when(k < comps)
        def _():
            advance(ITERS - 1, k)
            gram_of(k)

        @pl.when(k == comps - 1)
        def _():
            sum_start(0, fold(total_sum[0]))

        @pl.when(k >= LAG)
        def _():
            form_of(k - LAG)

        return 0

    lax.fori_loop(0, comps + LAG, last, 0)
    def cut(c, _):
        way = upward(c)
        side = jnp.where(way, 0, 1)
        x = jnp.where(way, 0, nx - 1)

        @pl.when(jnp.where(way, me[0], counts[0] - 1 - me[0]) > 0)
        def _():
            pltpu.make_async_remote_copy(
                src_ref=field.at[ITERS, c, 0],
                dst_ref=plane_in.at[ITERS + 1, c, side],
                send_sem=send_sem.at[ITERS, c, side],
                recv_sem=recv_sem.at[ITERS, c, side],
                device_id={"gx": me[0] + 1 - 2 * jnp.where(way, 1, 0)},
                device_id_type=MESH,
            ).wait_recv()
            there = plane_in[ITERS + 1, c, side] * (-2.0 * weights[c, x, side])
            high, low = split(there.reshape(tall, nz), 2)
            here = pl.ds(pl.multiple_of(x * nz, nz), nz)
            own = [parts[c, p, :, here] for p in range(2)]
            more = contract_last(own[0], high) + contract_last(own[1], high)
            total_sum[1] += more + contract_last(own[0], low)

        return 0

    lax.fori_loop(0, comps, cut, 0)
    sum_start(1, fold(total_sum[1]))
    gram = sum_end(0)
    mixing = inverse_factor(unpacked(gram) / total_rows, vecs)
    mixing_out[...] = mixing

    widen = jnp.where(
        lax.broadcasted_iota(jnp.int32, (vecs, tall), 0)
        == lax.broadcasted_iota(jnp.int32, (vecs, tall), 1) // ny,
        1.0,
        0.0,
    ).astype(BF16)
    same = (
        lax.broadcasted_iota(jnp.int32, (tall, tall), 0) % ny
        == lax.broadcasted_iota(jnp.int32, (tall, tall), 1) % ny
    )
    mixers = []
    for piece in split(mixing, 2):
        tallest = jnp.broadcast_to(piece.astype(F32)[:, None, :], (vecs, ny, vecs))
        big = matmul(tallest.reshape(tall, vecs).astype(BF16), widen)
        mixers.append(jnp.where(same, big, 0.0).astype(BF16))
    for p in range(2):
        image_parts[p, :, :tall] = mixers[p]

    def mix(c, _):
        for x in range(0, nx, 2):
            high, low = (parts[c, p, :, x * nz : (x + 2) * nz] for p in range(2))
            left = [image_parts[p, :, :tall] for p in range(2)]
            out = matmul(left[0], high) + matmul(left[1], high)
            out = out + matmul(left[0], low)
            for t in range(2):
                stage[c, :, x + t] = out[:, t * nz : (t + 1) * nz].reshape(vecs, ny, nz)
        return 0

    lax.fori_loop(0, comps, mix, 0)
    def sent(k, _):
        s, c = lax.div(k, comps), lax.rem(k, comps)
        for side in range(6):

            @pl.when(sends(s, c, side))
            def _(side=side):
                send_copy(s, c, side).wait_send()

        return 0

    lax.fori_loop(0, (ITERS + 1) * comps, sent, 0)
    for side in range(6):

        @pl.when(has(side))
        def _(side=side):
            phase_copy(side, side ^ 1).wait_send()

    each_other(lambda other: sum_copy(0, me, other).wait_send())
    form_out[...] = unpacked(sum_end(1))
    each_other(lambda other: sum_copy(1, me, other).wait_send())


def finish(total_rows, stage, mixing, form, basis, coarse, small, sem):
    copy = pltpu.make_async_copy(stage, basis, sem.at[0])
    copy.start()
    exact = lax.Precision.HIGHEST
    left = mixing[...]
    first = jnp.dot(left, form[...], precision=exact, preferred_element_type=F32)
    small[...] = (
        lax.dot_general(
            first,
            left,
            (((1,), (1,)), ((), ())),
            precision=exact,
            preferred_element_type=F32,
        )
        / total_rows
    )
    other = pltpu.make_async_copy(small, coarse, sem.at[1])
    other.start()
    other.wait()
    copy.wait()


def on_device(counts, phase, lame, start):
    comps, vecs, nx, ny, nz = dims = start.shape
    packs = 2 * vecs * nx // nz
    tall, wide = vecs * ny, nx * nz
    assert comps == 3 and nx % 2 == 0 and ny == 8 and nz % 128 == 0
    assert (nz // 2) % GROUP == 0 and vecs % PANEL == 0
    assert packs * nz == 2 * vecs * nx and vecs % (2 * packs) == 0
    slots = counts[0] * counts[1] * counts[2]
    steps = ITERS + 1
    total_rows = 1.0 * comps * nx * ny * nz * counts[0] * counts[1] * counts[2]
    hbm = pl.BlockSpec(memory_space=pltpu.HBM)
    vmem = pl.BlockSpec(memory_space=pltpu.VMEM)
    square = jax.ShapeDtypeStruct((vecs, vecs), F32)
    down = vecs // (nz // vecs)
    handed = pl.pallas_call(
        functools.partial(kernel, counts, dims),
        out_shape=(
            pltpu.VMEM(start.shape, F32),
            pltpu.VMEM((vecs, vecs), F32),
            pltpu.VMEM((vecs, vecs), F32),
        ),
        in_specs=[hbm, hbm, hbm],
        out_specs=(vmem, vmem, vmem),
        scratch_shapes=[
            pltpu.SMEM(lame.shape, F32),
            pltpu.VMEM(phase.shape, jnp.int32),
            pltpu.VMEM((steps + 1, comps, nx, vecs, ny, nz), F32),
            pltpu.VMEM((steps + 1, comps, 2, vecs, ny, nz), F32),
            pltpu.VMEM((steps, comps, 2, nx, vecs, nz), F32),
            pltpu.VMEM((steps + 1, comps, packs, ny, nz), F32),
            pltpu.VMEM((steps, comps, 2, packs, ny, nz), F32),
            pltpu.VMEM((6,) + phase.shape, jnp.int32),
            pltpu.VMEM((comps, nx, 7, ny, nz), F32),
            pltpu.VMEM((comps, 2, tall, wide), BF16),
            pltpu.VMEM((2, tall, max(wide, tall)), BF16),
            pltpu.VMEM((2, tall, tall), F32),
            pltpu.VMEM((2, slots, down, nz), F32),
            pltpu.SemaphoreType.DMA((comps * nx + 2,)),
            pltpu.SemaphoreType.DMA((6,)),
            pltpu.SemaphoreType.DMA((6,)),
            pltpu.SemaphoreType.DMA((steps, comps, 6)),
            pltpu.SemaphoreType.DMA((steps, comps, 6)),
            pltpu.SemaphoreType.DMA((2, slots)),
            pltpu.SemaphoreType.DMA((2, slots)),
        ],
        compiler_params=pltpu.CompilerParams(
            collective_id=0, has_side_effects=True, vmem_limit_bytes=62 * 2**20
        ),
    )(lame, phase, start)
    handed = [pltpu.with_memory_space_constraint(one, pltpu.VMEM) for one in handed]
    return pl.pallas_call(
        functools.partial(finish, total_rows),
        out_shape=(jax.ShapeDtypeStruct(start.shape, F32), square),
        in_specs=[vmem, vmem, vmem],
        out_specs=(hbm, hbm),
        scratch_shapes=[
            pltpu.VMEM((vecs, vecs), F32),
            pltpu.SemaphoreType.DMA((2,)),
        ],
        compiler_params=pltpu.CompilerParams(vmem_limit_bytes=4 * 2**20),
    )(*handed)


def solution(mesh):
    counts = tuple(mesh.shape[axis] for axis in AXES)
    spread = P(None, None, *AXES)
    return jax.shard_map(
        functools.partial(on_device, counts),
        mesh=mesh,
        in_specs=(P(*AXES), P(), spread),
        out_specs=(spread, P()),
        check_vma=False,
    )
```
